256 devices in a mesh: row: 16 (over x, y), col: 16 (over z, core).
Axes of the slice: x: 4, y: 4, z: 8, core: 2. Of those that a mesh axis runs over, the one named last changes fastest.
Arguments:
- tokens: bfloat16 [512, 8192], P('col', 'row'), may hold values from -6 to 6
- cotangent: bfloat16 [512, 8192], P('col', 'row'), may hold values from -6 to 6
- gate_weight: bfloat16 [8192, 32768], P('row', 'col'), may hold values from -0.125 to 0.125
- up_weight: bfloat16 [8192, 32768], P('row', 'col'), may hold values from -0.125 to 0.125
- down_weight: bfloat16 [32768, 8192], P('col', 'row'), may hold values from -0.0625 to 0.0625
- block_mask: int32 [3, 16, 64], P(None, 'row', 'col'), may hold values 0 or 1
Outputs:
- input_grad: bfloat16 [512, 8192], P('col', 'row')
- gate_grad: bfloat16 [8192, 32768], P('row', 'col')
- up_grad: bfloat16 [8192, 32768], P('row', 'col')
- down_grad: bfloat16 [32768, 8192], P('col', 'row')
The draws below stay inside these ranges and needn't reach their ends.
All inputs are finite; a program needn't handle non-finite values. No bound on the sum of `block_mask` on one device may be relied on, other than what follows from the above.
Results may differ from the reference program's by a relative error of at most 0.005.
Values may be sent and summed in bfloat16 or wider, within the bound.
No kernel may reach another device: no remote copies, remote signals or barrier semaphores. Data moves between devices by JAX's collectives and lax.ppermute only.
A program may use at most 128 MiB of HBM per device.

```python
import jax
import jax.numpy as jnp

D = 8192
FF = 32768
BLK = 512
TOKENS = 512
DB = 16
FB = 64


def place_ends(array, key, low, high):
    place = [jax.random.randint(jax.random.fold_in(key, axis), (), 0, length) for axis, length in enumerate(array.shape)]
    widest = array.shape.index(max(array.shape))
    beside = place[:widest] + [(place[widest] + 1) % array.shape[widest]] + place[widest + 1:]
    return array.at[tuple(place)].set(low).at[tuple(beside)].set(high)


def shard_levels(own_key, shape, shards, least, top_value):
    factor_of, own = 1.0, jax.random.fold_in(own_key, 6)
    for position, shards_of in shards:
        draws = jnp.exp(jax.random.uniform(jax.random.fold_in(own, position), (shards_of,), jnp.float32, least / len(shards), top_value / len(shards)))
        factor_of = factor_of * jnp.repeat(draws, shape[position] // shards_of).reshape([-1 if axis == position else 1 for axis in range(len(shape))])
    return factor_of


def normal_values(stream_key, dims, spread, reach, cuts=(), kind=jnp.bfloat16):
    result = jax.random.normal(stream_key, dims, jnp.float32) * spread
    if len(cuts) > 0:
        result = shard_levels(stream_key, dims, cuts, -0.22, 0.18) * result
    return jnp.clip(result, min=-reach, max=reach).astype(kind)


def setup_inputs(seed: int = 0) -> dict:
    arg_keys = jax.random.split(jax.random.key(seed), 7)
    tokens = normal_values(arg_keys[0], (TOKENS, D), 1.0, 6.0, ((0, 16), (1, 16)))
    cotangent = normal_values(arg_keys[1], (TOKENS, D), 1.0, 6.0, ((0, 16), (1, 16)))
    gate_weight = normal_values(arg_keys[2], (D, FF), (D // 4) ** -0.5, 0.125, ((0, 16), (1, 16)))
    up_weight = normal_values(arg_keys[3], (D, FF), (D // 4) ** -0.5, 0.125, ((0, 16), (1, 16)))
    down_weight = normal_values(arg_keys[4], (FF, D), (FF // 4) ** -0.5, 0.0625, ((0, 16), (1, 16)))
    block_mask = place_ends((jax.random.randint(arg_keys[5], (3, DB, FB), 0, 4) < 1).astype(jnp.int32), jax.random.fold_in(arg_keys[5], 1), 0, 1)
    return dict(tokens=tokens, cotangent=cotangent, gate_weight=gate_weight, up_weight=up_weight, down_weight=down_weight, block_mask=block_mask)


def expand(kept_map):
    return jnp.repeat(jnp.repeat(kept_map, BLK, axis=0), BLK, axis=1).astype(jnp.bfloat16)


def reference(tokens, cotangent, gate_weight, up_weight, down_weight, block_mask):
    mask_gate = expand(block_mask[0])
    mask_up = expand(block_mask[1])
    mask_down = expand(block_mask[2]).T
    kept_gate = gate_weight * mask_gate
    kept_up = up_weight * mask_up
    kept_down = down_weight * mask_down
    gate_value = jnp.dot(tokens, kept_gate, preferred_element_type=jnp.float32)
    up_value = jnp.dot(tokens, kept_up, preferred_element_type=jnp.float32)
    hidden_grad = jnp.dot(cotangent, kept_down.T, preferred_element_type=jnp.float32)
    sigmoid = jax.nn.sigmoid(gate_value)
    swish = gate_value * sigmoid
    hidden = (swish * up_value).astype(jnp.bfloat16)
    gate_delta = (hidden_grad * up_value * sigmoid * (1.0 + gate_value * (1.0 - sigmoid))).astype(jnp.bfloat16)
    up_delta = (hidden_grad * swish).astype(jnp.bfloat16)
    down_grad = (jnp.dot(hidden.T, cotangent, preferred_element_type=jnp.float32) * mask_down).astype(jnp.bfloat16)
    gate_grad = (jnp.dot(tokens.T, gate_delta, preferred_element_type=jnp.float32) * mask_gate).astype(jnp.bfloat16)
    up_grad = (jnp.dot(tokens.T, up_delta, preferred_element_type=jnp.float32) * mask_up).astype(jnp.bfloat16)
    input_grad = (jnp.dot(gate_delta, kept_gate.T, preferred_element_type=jnp.float32)
                  + jnp.dot(up_delta, kept_up.T, preferred_element_type=jnp.float32)).astype(jnp.bfloat16)
    return (input_grad, gate_grad, up_grad, down_grad)
```

```python
import jax
import jax.numpy as jnp
from jax import lax
from jax.experimental import pallas as pl
from jax.experimental.pallas import tpu as pltpu
from jax.sharding import Mesh, PartitionSpec as P


BLK = 512
F32 = jnp.float32
BF16 = jnp.bfloat16

RING = (0, 1, 3, 2)
PAIRS_LOW = [(0, 1), (1, 0), (2, 3), (3, 2)]
PAIRS_HIGH = [(1, 2), (2, 1), (3, 0), (0, 3)]
DIMS = (("x", PAIRS_LOW), ("x", PAIRS_HIGH), ("y", PAIRS_LOW), ("y", PAIRS_HIGH))
ORDERS = ((0, 1, 2, 3), (1, 0, 3, 2), (2, 3, 0, 1), (3, 2, 1, 0))
QUARTERS = len(ORDERS)
NODES = 16
GROUP = 8


def exchange(value, dim):
    axis, pairs = DIMS[dim]
    return lax.ppermute(value, axis, pairs)


def block_order(order):
    kept = [0]
    for dim in reversed(order):
        sent = [p ^ (1 << dim) for p in kept]
        kept = sent + kept
    return kept


def token_places(tokens):
    half = NODES // 2
    orders = [block_order(order) for order in ORDERS]
    places = [q * NODES + p for q in range(QUARTERS) for p in orders[q][:half]]
    places += [q * NODES + p for q in range(QUARTERS) for p in orders[q][half:]]
    return places


def dot(a, b, contract):
    return lax.dot_general(a, b, ((contract[:1], contract[1:]), ((), ())), preferred_element_type=F32)


def forward_kernel(mask, tok, cot, gate, up, down, *outs):
    m = pl.program_id(0)
    f = pl.program_id(1)
    rows = outs[0].shape[1]

    def put(value):
        for q, out in enumerate(outs):
            out[0] = value[q * rows : (q + 1) * rows].astype(out.dtype)

    keep = mask[m, f] != 0

    @pl.when(jnp.logical_not(keep))
    def _():
        for out in outs:
            out[...] = jnp.zeros_like(out)

    @pl.when(jnp.logical_and(keep, m == 0))
    def _():
        put(dot(tok[...], gate[...], (1, 0)))

    @pl.when(jnp.logical_and(keep, m == 1))
    def _():
        put(dot(tok[...], up[...], (1, 0)))

    @pl.when(jnp.logical_and(keep, m == 2))
    def _():
        put(dot(cot[...], down[...], (1, 1)))


def forward(mask, tok, cot, gate, up, down, dtype, name):
    rows, width = tok.shape
    hidden = gate.shape[1]
    nf = hidden // BLK
    last = nf - 1

    def turn(which):
        return lambda m, f: jnp.where(m == which, f, jnp.where(m < which, 0, last))

    gate_at, up_at, down_at = turn(0), turn(1), turn(2)
    return pl.pallas_call(
        forward_kernel,
        name=name,
        grid_spec=pltpu.PrefetchScalarGridSpec(
            num_scalar_prefetch=1,
            grid=(3, nf),
            in_specs=[
                pl.BlockSpec((rows, width), lambda m, f, mask: (0, 0)),
                pl.BlockSpec((rows, width), lambda m, f, mask: (0, 0)),
                pl.BlockSpec((width, BLK), lambda m, f, mask: (0, gate_at(m, f))),
                pl.BlockSpec((width, BLK), lambda m, f, mask: (0, up_at(m, f))),
                pl.BlockSpec((BLK, width), lambda m, f, mask: (down_at(m, f), 0)),
            ],
            out_specs=[pl.BlockSpec((1, rows // QUARTERS, BLK), lambda m, f, mask: (m, 0, f))] * QUARTERS,
        ),
        out_shape=[jax.ShapeDtypeStruct((3, rows // QUARTERS, hidden), dtype)] * QUARTERS,
        cost_estimate=pl.CostEstimate(
            flops=6 * rows * width * hidden,
            transcendentals=0,
            bytes_accessed=6 * width * hidden + 3 * rows * hidden * jnp.dtype(dtype).itemsize,
        ),
    )(mask, tok, cot, gate, up, down)


def backward_kernel(mask, places, tok, cot, gate, up, *refs):
    pieces = refs[: 2 * QUARTERS]
    gate_grad, up_grad, down_grad, input_grad, acc = refs[2 * QUARTERS :]
    f = pl.program_id(0)

    def whole(m):
        return jnp.concatenate([piece[m] for piece in pieces], axis=0)

    @pl.when(f == 0)
    def _():
        acc[...] = jnp.zeros_like(acc)

    def weight_part(m, weight, out):
        @pl.when(mask[m, f] != 0)
        def _():
            delta = whole(m + 1)
            out[...] = dot(tok[...], delta, (0, 0)).astype(out.dtype)
            acc[...] += dot(delta, weight[...], (1, 1))

        @pl.when(mask[m, f] == 0)
        def _():
            out[...] = jnp.zeros_like(out)

    weight_part(0, gate, gate_grad)
    weight_part(1, up, up_grad)

    @pl.when(mask[2, f] != 0)
    def _():
        down_grad[...] = dot(whole(0), cot[...], (0, 0)).astype(down_grad.dtype)

    @pl.when(mask[2, f] == 0)
    def _():
        down_grad[...] = jnp.zeros_like(down_grad)

    @pl.when(f == pl.num_programs(0) - 1)
    def _():
        for i in range(input_grad.shape[0]):
            input_grad[places[i]] = acc[i * GROUP : (i + 1) * GROUP]


def backward(mask, places, tok, cot, gate, up, pieces):
    rows, width = tok.shape
    hidden = gate.shape[1]
    groups = rows // GROUP
    share = pieces[0].shape[1]
    return pl.pallas_call(
        backward_kernel,
        name="backward",
        grid_spec=pltpu.PrefetchScalarGridSpec(
            num_scalar_prefetch=2,
            grid=(hidden // BLK,),
            in_specs=[
                pl.BlockSpec((rows, width), lambda f, *_: (0, 0)),
                pl.BlockSpec((rows, width), lambda f, *_: (0, 0)),
                pl.BlockSpec((width, BLK), lambda f, *_: (0, f)),
                pl.BlockSpec((width, BLK), lambda f, *_: (0, f)),
            ]
            + [pl.BlockSpec((3, share, BLK), lambda f, *_: (0, 0, f))] * len(pieces),
            out_specs=[
                pl.BlockSpec((width, BLK), lambda f, *_: (0, f)),
                pl.BlockSpec((width, BLK), lambda f, *_: (0, f)),
                pl.BlockSpec((BLK, width), lambda f, *_: (f, 0)),
                pl.BlockSpec((groups, GROUP, width), lambda f, *_: (0, 0, 0)),
            ],
            scratch_shapes=[pltpu.VMEM((rows, width), F32)],
        ),
        out_shape=[
            jax.ShapeDtypeStruct((width, hidden), BF16),
            jax.ShapeDtypeStruct((width, hidden), BF16),
            jax.ShapeDtypeStruct((hidden, width), BF16),
            jax.ShapeDtypeStruct((groups, GROUP, width), F32),
        ],
        cost_estimate=pl.CostEstimate(
            flops=10 * rows * width * hidden,
            transcendentals=0,
            bytes_accessed=10 * width * hidden + 6 * rows * hidden,
        ),
    )(mask, places, tok, cot, gate, up, *pieces)


def swiglu(shares):
    gate_value, up_value, hidden_grad = shares[0], shares[1], shares[2]
    sigmoid = jax.nn.sigmoid(gate_value)
    swish = gate_value * sigmoid
    hidden = (swish * up_value).astype(BF16)
    gate_delta = (hidden_grad * up_value * sigmoid * (1.0 + gate_value * (1.0 - sigmoid))).astype(BF16)
    up_delta = (hidden_grad * swish).astype(BF16)
    return jnp.stack([hidden, gate_delta, up_delta])


def reduce_rows(sent, kept, order):
    received = exchange(sent, order[0]).astype(F32)
    half = kept.shape[1] // 2
    received = exchange((kept[:, :half] + received[:, :half]).astype(BF16), order[1]).astype(F32) + (
        kept[:, half:] + received[:, half:]
    )
    for dim in order[2:]:
        half = received.shape[1] // 2
        received = received[:, half:] + exchange(received[:, :half], dim)
    return received


def gather_rows(own, order):
    for dim in reversed(order[1:]):
        own = jnp.concatenate([exchange(own, dim), own], axis=1)
    return exchange(own, order[0]), own


def shards(tokens, cotangent, gate_weight, up_weight, down_weight, block_mask):
    depth = lax.axis_size("z")
    mine, width = tokens.shape
    mask = block_mask.reshape(3, -1)
    ring = jnp.array(RING, jnp.int32)
    bits = ring[lax.axis_index("x")] + 4 * ring[lax.axis_index("y")]
    other_core = [(0, 1), (1, 0)]

    both = jnp.concatenate([tokens, cotangent], axis=1)
    z = lax.axis_index("z")
    column = lax.all_to_all(jnp.broadcast_to(both[None], (depth,) + both.shape), "z", 0, 0)
    column = column.reshape(depth * mine, 2 * width)
    gathered = jnp.concatenate([column, lax.ppermute(column, "core", other_core)], axis=0)

    count = gathered.shape[0]
    places = jnp.bitwise_xor(jnp.array(token_places(count), jnp.int32), bits)
    source = jnp.repeat(places, GROUP) * GROUP + jnp.tile(jnp.arange(GROUP, dtype=jnp.int32), count // GROUP)
    select = (source[:, None] == jnp.arange(count, dtype=jnp.int32)[None]).astype(BF16)
    permuted = jnp.dot(select, gathered, preferred_element_type=F32).astype(BF16)
    tok, cot = permuted[:, :width], permuted[:, width:]

    half = count // 2
    weights = (gate_weight, up_weight, down_weight)
    sent = forward(mask, tok[:half], cot[:half], *weights, BF16, "forward_sent")
    kept = forward(mask, tok[half:], cot[half:], *weights, F32, "forward_kept")

    summed = [reduce_rows(sent[q], kept[q], ORDERS[q]) for q in range(QUARTERS)]
    gained = [gather_rows(swiglu(summed[q]), ORDERS[q]) for q in range(QUARTERS)]
    pieces = [far for far, _ in gained] + [near for _, near in gained]

    gate_grad, up_grad, down_grad, input_grad = backward(
        mask, places, tok, cot, gate_weight, up_weight, pieces
    )
    input_grad = input_grad.reshape(2, depth, mine, width)
    input_grad = input_grad[0] + lax.ppermute(input_grad[1], "core", other_core)
    parts = lax.all_to_all(input_grad.astype(BF16), "z", 0, 0)
    input_grad = jnp.sum(parts.astype(F32), axis=0)
    return (input_grad.astype(BF16), gate_grad, up_grad, down_grad)


def solution(mesh):
    torus = Mesh(mesh.devices.reshape(4, 4, -1, 2), ("x", "y", "z", "core"))
    row, col = ("x", "y"), ("z", "core")
    in_specs = (P(col, row), P(col, row), P(row, col), P(row, col), P(col, row), P(None, row, col))
    out_specs = (P(col, row), P(row, col), P(row, col), P(col, row))
    return jax.shard_map(shards, mesh=torus, in_specs=in_specs, out_specs=out_specs, check_vma=False)
```

```python
import jax
import jax.numpy as jnp
from jax import lax
from jax.experimental import pallas as pl
from jax.experimental.pallas import tpu as pltpu
from jax.sharding import Mesh, PartitionSpec as P


BLK = 512
VMEM_LIMIT = 20 * 2**20
F32 = jnp.float32
BF16 = jnp.bfloat16

PAIRS_LOW = [(0, 1), (1, 0), (2, 3), (3, 2)]
PAIRS_HIGH = [(1, 2), (2, 1), (3, 0), (0, 3)]
DIMS = (("x", PAIRS_LOW), ("x", PAIRS_HIGH), ("y", PAIRS_LOW), ("y", PAIRS_HIGH))
ORDERS = ((0, 1, 2, 3), (1, 0, 3, 2), (2, 3, 0, 1), (3, 2, 1, 0))
QUARTERS = len(ORDERS)
NODES = 16
GROUP = 8


def exchange(value, dim):
    axis, pairs = DIMS[dim]
    return lax.ppermute(value, axis, pairs)


def block_order(order):
    kept = [0]
    for dim in reversed(order):
        sent = [p ^ (1 << dim) for p in kept]
        kept = sent + kept
    return kept


def token_places():
    half = NODES // 2
    orders = [block_order(order) for order in ORDERS]
    places = [q * NODES + p for q in range(QUARTERS) for p in orders[q][:half]]
    places += [q * NODES + p for q in range(QUARTERS) for p in orders[q][half:]]
    return places


def dot(a, b, contract):
    return lax.dot_general(a, b, ((contract[:1], contract[1:]), ((), ())), preferred_element_type=F32)


def forward_kernel(mask, tok, cot, gate, up, down, *refs):
    outs = refs[:QUARTERS]
    buffers, sems = refs[QUARTERS:-1], refs[-1]
    f = pl.program_id(0)
    rows = outs[0].shape[1]

    def fetch(m, at):
        cut = pl.ds(at * BLK, BLK)
        source = (gate.at[:, cut], up.at[:, cut], down.at[cut, :])[m]
        return pltpu.make_async_copy(source, buffers[m].at[at], sems.at[m, at])

    @pl.when(f == 0)
    def _():
        for at in range(buffers[0].shape[0]):
            for m in range(3):
                fetch(m, at).start()

    for m, (value, contract) in enumerate(((tok, (1, 0)), (tok, (1, 0)), (cot, (1, 1)))):
        fetch(m, f).wait()

        @pl.when(mask[m, f] != 0)
        def _():
            product = dot(value[...], buffers[m][f], contract)
            for q, out in enumerate(outs):
                out[m] = product[q * rows : (q + 1) * rows].astype(out.dtype)

        @pl.when(mask[m, f] == 0)
        def _():
            for out in outs:
                out[m] = jnp.zeros(out.shape[1:], out.dtype)


def forward(mask, permuted, half, gate, up, down, dtype):
    count, both = permuted.shape
    rows, width = count // 2, both // 2
    hidden = gate.shape[1]
    blocks = hidden // BLK
    share = rows // QUARTERS
    return pl.pallas_call(
        forward_kernel,
        grid_spec=pltpu.PrefetchScalarGridSpec(
            num_scalar_prefetch=1,
            grid=(blocks,),
            in_specs=[
                pl.BlockSpec((rows, width), lambda f, mask: (half, 0)),
                pl.BlockSpec((rows, width), lambda f, mask: (half, 1)),
            ]
            + [pl.BlockSpec(memory_space=pl.ANY)] * 3,
            out_specs=[pl.BlockSpec((3, share, BLK), lambda f, mask: (0, 0, f))] * QUARTERS,
            scratch_shapes=[
                pltpu.VMEM((blocks, width, BLK), BF16),
                pltpu.VMEM((blocks, width, BLK), BF16),
                pltpu.VMEM((blocks, BLK, width), BF16),
                pltpu.SemaphoreType.DMA((3, blocks)),
            ],
        ),
        out_shape=[jax.ShapeDtypeStruct((3, share, hidden), dtype)] * QUARTERS,
        compiler_params=pltpu.CompilerParams(vmem_limit_bytes=VMEM_LIMIT),
        cost_estimate=pl.CostEstimate(
            flops=6 * rows * width * hidden,
            transcendentals=0,
            bytes_accessed=6 * width * hidden + 3 * rows * hidden * jnp.dtype(dtype).itemsize,
        ),
    )(mask, permuted, permuted, gate, up, down)


def whole(far, near, m_far, m_near):
    return jnp.concatenate([piece[m_far] for piece in far] + [piece[m_near] for piece in near], axis=0)


def input_kernel(mask, places, gate, up, *refs):
    far, near = refs[:QUARTERS], refs[QUARTERS : 2 * QUARTERS]
    input_grad, acc = refs[2 * QUARTERS :]
    f = pl.program_id(0)

    @pl.when(f == 0)
    def _():
        acc[...] = jnp.zeros_like(acc)

    for m, weight in enumerate((gate, up)):

        @pl.when(mask[m, f] != 0)
        def _():
            acc[...] += dot(whole(far, near, m, m), weight[...], (1, 1))

    @pl.when(f == pl.num_programs(0) - 1)
    def _():
        for i in range(input_grad.shape[0]):
            input_grad[places[i]] = acc[i * GROUP : (i + 1) * GROUP]


def input_gradient(mask, places, gate, up, far, near):
    width, hidden = gate.shape
    share = near[0].shape[1]
    rows = 2 * QUARTERS * share
    groups = rows // GROUP
    return pl.pallas_call(
        input_kernel,
        name="input_gradient",
        grid_spec=pltpu.PrefetchScalarGridSpec(
            num_scalar_prefetch=2,
            grid=(hidden // BLK,),
            in_specs=[pl.BlockSpec((width, BLK), lambda f, *_: (0, f))] * 2
            + [pl.BlockSpec((2, share, BLK), lambda f, *_: (0, 0, f))] * QUARTERS
            + [pl.BlockSpec((3, share, BLK), lambda f, *_: (0, 0, f))] * QUARTERS,
            out_specs=pl.BlockSpec((groups, GROUP, width), lambda f, *_: (0, 0, 0)),
            scratch_shapes=[pltpu.VMEM((rows, width), F32)],
        ),
        out_shape=jax.ShapeDtypeStruct((groups, GROUP, width), F32),
        compiler_params=pltpu.CompilerParams(vmem_limit_bytes=VMEM_LIMIT),
        cost_estimate=pl.CostEstimate(
            flops=4 * rows * width * hidden,
            transcendentals=0,
            bytes_accessed=4 * width * hidden + 5 * rows * hidden + 4 * rows * width,
        ),
    )(mask, places, gate, up, *far, *near)


def weight_kernel(mask, tok, cot, *refs):
    far, far_hidden, near = (refs[i * QUARTERS : (i + 1) * QUARTERS] for i in range(3))
    gate_grad, up_grad, down_grad = refs[3 * QUARTERS :]
    f = pl.program_id(0)

    def put(m, out, product):
        @pl.when(mask[m, f] != 0)
        def _():
            out[...] = product().astype(out.dtype)

        @pl.when(mask[m, f] == 0)
        def _():
            out[...] = jnp.zeros_like(out)

    put(0, gate_grad, lambda: dot(tok[...], whole(far, near, 0, 0), (0, 0)))
    put(1, up_grad, lambda: dot(tok[...], whole(far, near, 1, 1), (0, 0)))
    put(2, down_grad, lambda: dot(whole(far_hidden, near, 0, 2), cot[...], (0, 0)))


def weight_gradients(mask, permuted, far, far_hidden, near):
    rows, both = permuted.shape
    width = both // 2
    share, hidden = near[0].shape[1:]
    return pl.pallas_call(
        weight_kernel,
        name="weight_gradients",
        grid_spec=pltpu.PrefetchScalarGridSpec(
            num_scalar_prefetch=1,
            grid=(hidden // BLK,),
            in_specs=[
                pl.BlockSpec((rows, width), lambda f, *_: (0, 0)),
                pl.BlockSpec((rows, width), lambda f, *_: (0, 1)),
            ]
            + [pl.BlockSpec((2, share, BLK), lambda f, *_: (0, 0, f))] * QUARTERS
            + [pl.BlockSpec((1, share, BLK), lambda f, *_: (0, 0, f))] * QUARTERS
            + [pl.BlockSpec((3, share, BLK), lambda f, *_: (0, 0, f))] * QUARTERS,
            out_specs=[
                pl.BlockSpec((width, BLK), lambda f, *_: (0, f)),
                pl.BlockSpec((width, BLK), lambda f, *_: (0, f)),
                pl.BlockSpec((BLK, width), lambda f, *_: (f, 0)),
            ],
        ),
        out_shape=[
            jax.ShapeDtypeStruct((width, hidden), BF16),
            jax.ShapeDtypeStruct((width, hidden), BF16),
            jax.ShapeDtypeStruct((hidden, width), BF16),
        ],
        compiler_params=pltpu.CompilerParams(vmem_limit_bytes=VMEM_LIMIT),
        cost_estimate=pl.CostEstimate(
            flops=6 * rows * width * hidden,
            transcendentals=0,
            bytes_accessed=6 * width * hidden + 6 * rows * hidden,
        ),
    )(mask, permuted, permuted, *far, *far_hidden, *near)


def swiglu(shares):
    gate_value, up_value, hidden_grad = shares[0], shares[1], shares[2]
    sigmoid = jax.nn.sigmoid(gate_value)
    swish = gate_value * sigmoid
    hidden = (swish * up_value).astype(BF16)
    gate_delta = (hidden_grad * up_value * sigmoid * (1.0 + gate_value * (1.0 - sigmoid))).astype(BF16)
    up_delta = (hidden_grad * swish).astype(BF16)
    return jnp.stack([gate_delta, up_delta, hidden])


def reduce_rows(sent, kept, order):
    received = exchange(sent, order[0])
    half = kept.shape[1] // 2
    passed = (kept[:, :half] + received[:, :half].astype(F32)).astype(BF16)
    held = exchange(passed, order[1]).astype(F32) + (kept[:, half:] + received[:, half:].astype(F32))
    for dim in order[2:]:
        half = held.shape[1] // 2
        held = held[:, half:] + exchange(held[:, :half], dim)
    return held


def gather_rows(own, order):
    for dim in reversed(order[1:]):
        own = jnp.concatenate([exchange(own, dim), own], axis=1)
    return own


def layer(tokens, cotangent, gate_weight, up_weight, down_weight, block_mask):
    depth = lax.axis_size("z")
    mine, width = tokens.shape
    mask = block_mask.reshape(3, -1)
    x, y = lax.axis_index("x"), lax.axis_index("y")
    bits = (x ^ (x >> 1)) + 4 * (y ^ (y >> 1))
    other_core = [(0, 1), (1, 0)]

    both = jnp.concatenate([tokens, cotangent], axis=1)
    column = lax.all_to_all(jnp.broadcast_to(both[None], (depth,) + both.shape), "z", 0, 0)
    column = column.reshape(depth * mine, 2 * width)
    gathered = jnp.concatenate([column, lax.ppermute(column, "core", other_core)], axis=0)

    count = gathered.shape[0]
    places = jnp.bitwise_xor(jnp.array(token_places(), jnp.int32), bits)
    source = jnp.repeat(places, GROUP) * GROUP + jnp.tile(jnp.arange(GROUP, dtype=jnp.int32), count // GROUP)
    select = (source[:, None] == jnp.arange(count, dtype=jnp.int32)[None]).astype(BF16)
    permuted = jnp.dot(select, gathered, preferred_element_type=F32).astype(BF16)

    weights = (gate_weight, up_weight, down_weight)
    sent = forward(mask, permuted, 0, *weights, BF16)
    kept = forward(mask, permuted, 1, *weights, F32)

    summed = [reduce_rows(sent[q], kept[q], ORDERS[q]) for q in range(QUARTERS)]
    near = [gather_rows(swiglu(summed[q]), ORDERS[q]) for q in range(QUARTERS)]
    far = [exchange(near[q][:2], ORDERS[q][0]) for q in range(QUARTERS)]
    far_hidden = [exchange(near[q][2:], ORDERS[q][0]) for q in range(QUARTERS)]
    input_grad = input_gradient(mask, places, gate_weight, up_weight, far, near)
    gate_grad, up_grad, down_grad = weight_gradients(mask, permuted, far, far_hidden, near)
    input_grad = input_grad.reshape(2, depth, mine, width)
    input_grad = input_grad[0] + lax.ppermute(input_grad[1], "core", other_core)
    parts = lax.all_to_all(input_grad.astype(BF16), "z", 0, 0)
    input_grad = jnp.sum(parts.astype(F32), axis=0)
    return (input_grad.astype(BF16), gate_grad, up_grad, down_grad)


def solution(mesh):
    torus = Mesh(mesh.devices.reshape(4, 4, -1, 2), ("x", "y", "z", "core"))
    row, col = ("x", "y"), ("z", "core")
    in_specs = (P(col, row), P(col, row), P(row, col), P(row, col), P(col, row), P(None, row, col))
    out_specs = (P(col, row), P(row, col), P(row, col), P(col, row))
    return jax.shard_map(layer, mesh=torus, in_specs=in_specs, out_specs=out_specs, check_vma=False)
```

```python
import jax
import jax.numpy as jnp
from jax import lax
from jax.experimental import pallas as pl
from jax.experimental.pallas import tpu as pltpu
from jax.sharding import Mesh, PartitionSpec as P


BLK = 512
VMEM_LIMIT = 20 * 2**20
F32 = jnp.float32
BF16 = jnp.bfloat16

FLIP = ((1, 0, 3, 2), (3, 2, 1, 0))
ORDERS = (((0, 1, 2, 3), (1, 0, 3, 2)), ((2, 3, 0, 1), (3, 2, 1, 0)))
CHAINS = 2
PIECES = 4
NODES = 16
GROUP = 16


def exchange(value, chain, step):
    pairs = []
    for x in range(4):
        for y in range(4):
            for core in range(2):
                dim = ORDERS[core][chain][step]
                to_x, to_y = (FLIP[dim][x], y) if dim < 2 else (x, FLIP[dim - 2][y])
                pairs.append((x * 8 + y * 2 + core, to_x * 8 + to_y * 2 + core))
    return lax.ppermute(value, ("x", "y", "core"), pairs)


def block_order(order):
    kept = [0]
    for dim in reversed(order):
        sent = [p ^ (1 << dim) for p in kept]
        kept = sent + kept
    return kept


def token_places(core):
    half = NODES // 2
    orders = [block_order(order) for order in ORDERS[core]]
    places = [chain * NODES + p for chain in range(CHAINS) for p in orders[chain][:half]]
    places += [chain * NODES + p for chain in range(CHAINS) for p in orders[chain][half:]]
    return places


def dot(a, b, contract):
    return lax.dot_general(a, b, ((contract[:1], contract[1:]), ((), ())), preferred_element_type=F32)


def forward_kernel(mask, tok, cot, gate, up, down, *refs):
    outs = refs[:PIECES]
    buffers, sems = refs[PIECES:-1], refs[-1]
    f = pl.program_id(0)
    rows = outs[0].shape[1]

    def fetch(m, at):
        cut = pl.ds(at * BLK, BLK)
        source = (gate.at[:, cut], up.at[:, cut], down.at[cut, :])[m]
        return pltpu.make_async_copy(source, buffers[m].at[at], sems.at[m, at])

    @pl.when(f == 0)
    def _():
        for at in range(buffers[0].shape[0]):
            for m in range(3):
                fetch(m, at).start()

    for m, (value, contract) in enumerate(((tok, (1, 0)), (tok, (1, 0)), (cot, (1, 1)))):
        fetch(m, f).wait()

        @pl.when(mask[m, f] != 0)
        def _():
            product = dot(value[...], buffers[m][f], contract)
            for q, out in enumerate(outs):
                out[m] = product[q * rows : (q + 1) * rows].astype(out.dtype)

        @pl.when(mask[m, f] == 0)
        def _():
            for out in outs:
                out[m] = jnp.zeros(out.shape[1:], out.dtype)


def forward(mask, permuted, half, gate, up, down, dtype):
    count, both = permuted.shape
    rows, width = count // 2, both // 2
    hidden = gate.shape[1]
    blocks = hidden // BLK
    share = rows // PIECES
    return pl.pallas_call(
        forward_kernel,
        grid_spec=pltpu.PrefetchScalarGridSpec(
            num_scalar_prefetch=1,
            grid=(blocks,),
            in_specs=[
                pl.BlockSpec((rows, width), lambda f, mask: (half, 0)),
                pl.BlockSpec((rows, width), lambda f, mask: (half, 1)),
            ]
            + [pl.BlockSpec(memory_space=pl.ANY)] * 3,
            out_specs=[pl.BlockSpec((3, share, BLK), lambda f, mask: (0, 0, f))] * PIECES,
            scratch_shapes=[
                pltpu.VMEM((blocks, width, BLK), BF16),
                pltpu.VMEM((blocks, width, BLK), BF16),
                pltpu.VMEM((blocks, BLK, width), BF16),
                pltpu.SemaphoreType.DMA((3, blocks)),
            ],
        ),
        out_shape=[jax.ShapeDtypeStruct((3, share, hidden), dtype)] * PIECES,
        compiler_params=pltpu.CompilerParams(vmem_limit_bytes=VMEM_LIMIT),
        cost_estimate=pl.CostEstimate(
            flops=6 * rows * width * hidden,
            transcendentals=0,
            bytes_accessed=6 * width * hidden + 3 * rows * hidden * jnp.dtype(dtype).itemsize,
        ),
    )(mask, permuted, permuted, gate, up, down)


def whole(far, near, m_far, m_near):
    return jnp.concatenate([piece[m_far] for piece in far] + [piece[m_near] for piece in near], axis=0)


def input_kernel(mask, places, gate, up, *refs):
    far, near = refs[:PIECES], refs[PIECES : 2 * PIECES]
    input_grad, acc = refs[2 * PIECES :]
    f = pl.program_id(0)

    @pl.when(f == 0)
    def _():
        acc[...] = jnp.zeros_like(acc)

    for m, weight in enumerate((gate, up)):

        @pl.when(mask[m, f] != 0)
        def _():
            acc[...] += dot(whole(far, near, m, m), weight[...], (1, 1))

    @pl.when(f == pl.num_programs(0) - 1)
    def _():
        for i in range(input_grad.shape[0]):
            input_grad[places[i]] = acc[i * GROUP : (i + 1) * GROUP]


def input_gradient(mask, places, gate, up, far, near):
    width, hidden = gate.shape
    share = near[0].shape[1]
    rows = 2 * PIECES * share
    groups = rows // GROUP
    return pl.pallas_call(
        input_kernel,
        name="input_gradient",
        grid_spec=pltpu.PrefetchScalarGridSpec(
            num_scalar_prefetch=2,
            grid=(hidden // BLK,),
            in_specs=[pl.BlockSpec((width, BLK), lambda f, *_: (0, f))] * 2
            + [pl.BlockSpec((2, share, BLK), lambda f, *_: (0, 0, f))] * PIECES
            + [pl.BlockSpec((3, share, BLK), lambda f, *_: (0, 0, f))] * PIECES,
            out_specs=pl.BlockSpec((groups, GROUP, width), lambda f, *_: (0, 0, 0)),
            scratch_shapes=[pltpu.VMEM((rows, width), F32)],
        ),
        out_shape=jax.ShapeDtypeStruct((groups, GROUP, width), F32),
        compiler_params=pltpu.CompilerParams(vmem_limit_bytes=VMEM_LIMIT),
        cost_estimate=pl.CostEstimate(
            flops=4 * rows * width * hidden,
            transcendentals=0,
            bytes_accessed=4 * width * hidden + 5 * rows * hidden + 4 * rows * width,
        ),
    )(mask, places, gate, up, *far, *near)


def weight_kernel(mask, tok, cot, *refs):
    far, far_hidden, near = (refs[i * PIECES : (i + 1) * PIECES] for i in range(3))
    gate_grad, up_grad, down_grad = refs[3 * PIECES :]
    f = pl.program_id(0)

    def put(m, out, product):
        @pl.when(mask[m, f] != 0)
        def _():
            out[...] = product().astype(out.dtype)

        @pl.when(mask[m, f] == 0)
        def _():
            out[...] = jnp.zeros_like(out)

    put(0, gate_grad, lambda: dot(tok[...], whole(far, near, 0, 0), (0, 0)))
    put(1, up_grad, lambda: dot(tok[...], whole(far, near, 1, 1), (0, 0)))
    put(2, down_grad, lambda: dot(whole(far_hidden, near, 0, 2), cot[...], (0, 0)))


def weight_gradients(mask, permuted, far, far_hidden, near):
    rows, both = permuted.shape
    width = both // 2
    share, hidden = near[0].shape[1:]
    return pl.pallas_call(
        weight_kernel,
        name="weight_gradients",
        grid_spec=pltpu.PrefetchScalarGridSpec(
            num_scalar_prefetch=1,
            grid=(hidden // BLK,),
            in_specs=[
                pl.BlockSpec((rows, width), lambda f, *_: (0, 0)),
                pl.BlockSpec((rows, width), lambda f, *_: (0, 1)),
            ]
            + [pl.BlockSpec((2, share, BLK), lambda f, *_: (0, 0, f))] * PIECES
            + [pl.BlockSpec((1, share, BLK), lambda f, *_: (0, 0, f))] * PIECES
            + [pl.BlockSpec((3, share, BLK), lambda f, *_: (0, 0, f))] * PIECES,
            out_specs=[
                pl.BlockSpec((width, BLK), lambda f, *_: (0, f)),
                pl.BlockSpec((width, BLK), lambda f, *_: (0, f)),
                pl.BlockSpec((BLK, width), lambda f, *_: (f, 0)),
            ],
        ),
        out_shape=[
            jax.ShapeDtypeStruct((width, hidden), BF16),
            jax.ShapeDtypeStruct((width, hidden), BF16),
            jax.ShapeDtypeStruct((hidden, width), BF16),
        ],
        compiler_params=pltpu.CompilerParams(vmem_limit_bytes=VMEM_LIMIT),
        cost_estimate=pl.CostEstimate(
            flops=6 * rows * width * hidden,
            transcendentals=0,
            bytes_accessed=6 * width * hidden + 6 * rows * hidden,
        ),
    )(mask, permuted, permuted, *far, *far_hidden, *near)


def swiglu(shares):
    gate_value, up_value, hidden_grad = shares[0], shares[1], shares[2]
    sigmoid = jax.nn.sigmoid(gate_value)
    swish = gate_value * sigmoid
    hidden = (swish * up_value).astype(BF16)
    gate_delta = (hidden_grad * up_value * sigmoid * (1.0 + gate_value * (1.0 - sigmoid))).astype(BF16)
    up_delta = (hidden_grad * swish).astype(BF16)
    return jnp.stack([gate_delta, up_delta, hidden])


def reduce_rows(sent, kept):
    chains = range(CHAINS)
    ahead = [exchange(sent[2 * c], c, 0) for c in chains]
    rest = [exchange(sent[2 * c + 1], c, 0) for c in chains]
    half = ahead[0].shape[1] // 2
    quarter = half // 2
    passed = [(kept[2 * c] + ahead[c].astype(F32)).astype(BF16) for c in chains]
    ahead = [exchange(passed[c][:, :half], c, 1) for c in chains]
    last = [exchange(passed[c][:, half:], c, 1) for c in chains]
    summed = []
    for c in chains:
        own, got = kept[2 * c + 1], rest[c]
        third = own[:, :half] + got[:, :half].astype(F32) + ahead[c].astype(F32)
        held = own[:, half:] + got[:, half:].astype(F32) + last[c].astype(F32)
        held = held + exchange(third, c, 2)
        summed.append(held[:, quarter:] + exchange(held[:, :quarter], c, 3))
    return summed


def gather_rows(own):
    near = []
    for c in range(CHAINS):
        rows = own[c]
        for step in (3, 2):
            rows = jnp.concatenate([exchange(rows, c, step), rows], axis=1)
        near += [exchange(rows, c, 1), rows]
    return near


def layer(tokens, cotangent, gate_weight, up_weight, down_weight, block_mask):
    depth = lax.axis_size("z")
    mine, width = tokens.shape
    mask = block_mask.reshape(3, -1)
    x, y = lax.axis_index("x"), lax.axis_index("y")
    bits = (x ^ (x >> 1)) + 4 * (y ^ (y >> 1))
    other_core = [(0, 1), (1, 0)]

    both = jnp.concatenate([tokens, cotangent], axis=1)
    column = lax.all_to_all(jnp.broadcast_to(both[None], (depth,) + both.shape), "z", 0, 0)
    column = column.reshape(depth * mine, 2 * width)
    gathered = jnp.concatenate([column, lax.ppermute(column, "core", other_core)], axis=0)

    count = gathered.shape[0]
    core = lax.axis_index("core")
    places = jnp.where(core == 0, *(jnp.array(token_places(c), jnp.int32) for c in range(2))) ^ bits
    source = jnp.repeat(places, GROUP) * GROUP + jnp.tile(jnp.arange(GROUP, dtype=jnp.int32), count // GROUP)
    select = (source[:, None] == jnp.arange(count, dtype=jnp.int32)[None]).astype(BF16)
    permuted = jnp.dot(select, gathered, preferred_element_type=F32).astype(BF16)

    weights = (gate_weight, up_weight, down_weight)
    sent = forward(mask, permuted, 0, *weights, BF16)
    kept = forward(mask, permuted, 1, *weights, F32)

    near = gather_rows([swiglu(shares) for shares in reduce_rows(sent, kept)])
    rest = [exchange(near[2 * c + 1][:2], c, 0) for c in range(CHAINS)]
    ahead = [exchange(near[2 * c][:2], c, 0) for c in range(CHAINS)]
    far = [piece for c in range(CHAINS) for piece in (ahead[c], rest[c])]
    far_hidden = [exchange(near[i][2:], i // 2, 0) for i in range(PIECES)]
    input_grad = input_gradient(mask, places, gate_weight, up_weight, far, near)
    gate_grad, up_grad, down_grad = weight_gradients(mask, permuted, far, far_hidden, near)
    input_grad = input_grad.reshape(2, depth, mine, width)
    input_grad = input_grad[0] + lax.ppermute(input_grad[1], "core", other_core)
    parts = lax.all_to_all(input_grad.astype(BF16), "z", 0, 0)
    input_grad = jnp.sum(parts.astype(F32), axis=0)
    return (input_grad.astype(BF16), gate_grad, up_grad, down_grad)


def solution(mesh):
    torus = Mesh(mesh.devices.reshape(4, 4, -1, 2), ("x", "y", "z", "core"))
    row, col = ("x", "y"), ("z", "core")
    in_specs = (P(col, row), P(col, row), P(row, col), P(row, col), P(col, row), P(None, row, col))
    out_specs = (P(col, row), P(row, col), P(row, col), P(col, row))
    return jax.shard_map(layer, mesh=torus, in_specs=in_specs, out_specs=out_specs, check_vma=False)
```
